32 devices in a mesh: elem: 8 (over y, x, core), mode: 4 (over z).
Axes of the slice: x: 2, y: 2, z: 4, core: 2. Of those that a mesh axis runs over, the one named last changes fastest.
Arguments:
- velocity: float32 [3, 5184, 2, 512], P(None, 'elem', None, 'mode'), may hold values from -3 to 3
- column_width: float32 [8], P('elem'), may hold values from 0.5 to 2
- row_height: float32 [8], replicated, may hold values from 0.5 to 2
- disc_mask: int32 [64], P('elem'), may hold values from 0 to 1, as said below
Outputs:
- velocity_new: float32 [3, 5184, 2, 512], P(None, 'elem', None, 'mode')
The draws below stay inside these ranges and needn't reach their ends.
Inputs may be any that keep to these rules, and one draw needn't show every extreme that they name: `disc_mask`: in each column of 8 elements the ones form one run of 2 to 4 consecutive rows, counted cyclically in y.
All inputs are finite; a program needn't handle non-finite values.
Results may differ from the reference program's by a relative error of at most 0.0001.
Values sent between devices are 32-bit elements; how exact they have to be, the bound alone decides.
A program may use at most 128 MiB of HBM per device.

```python
import math
import jax
import jax.numpy as jnp
import numpy as np
from jax import lax

ORDER = 8
MODES = 512
E_DEV = 8
ITERS = 2
COLS = 8
ELEMS = 64
NODES = 5184


def draw_disc_mask(key, part):
    key_start, key_length = jax.random.split(key)
    starts = jax.random.randint(key_start, (COLS,), 0, E_DEV)
    lengths = jax.random.randint(key_length, (COLS,), 2, 5)
    column_index = jnp.arange(COLS)
    lengths = jnp.where(column_index == 0, 4, jnp.where(column_index == 1, 2, lengths))
    row_index = jnp.arange(E_DEV)
    marked = (row_index[None, :] - starts[:, None]) % E_DEV < lengths[:, None]
    return marked.astype(jnp.int32).reshape(ELEMS)


def steps_of(rng, shape, shards, low, high):
    loudness, own = 1.0, jax.random.fold_in(rng, 6)
    for position, blocks in shards:
        heights = jnp.exp(jax.random.uniform(jax.random.fold_in(own, position), (blocks,), jnp.float32, low / len(shards), high / len(shards)))
        loudness = loudness * jnp.repeat(heights, shape[position] // blocks).reshape([-1 if axis == position else 1 for axis in range(len(shape))])
    return loudness


def gaussian(own_key, dims, scale, reach, cuts=(), held_as=jnp.bfloat16):
    values = jax.random.normal(own_key, dims, jnp.float32) * scale
    if len(cuts) > 0:
        values = steps_of(own_key, dims, cuts, -0.22, 0.18) * values
    return jnp.clip(values, min=-reach, max=reach).astype(held_as)


def setup_inputs(seed: int = 0) -> dict:
    key_of = jax.random.split(jax.random.key(seed), 5)
    velocity = gaussian(key_of[0], (3, NODES, 2, MODES), 0.5, 3.0, ((1, 8), (3, 4)), jnp.float32)
    column_width = jnp.clip(jnp.exp(math.log(2.0) - 1.3862944 * jax.random.uniform(key_of[1], (COLS,), jnp.float32) ** steps_of(key_of[1], (COLS,), ((0, 8),), -0.2, 0.2)), 0.5, 2.0)
    row_height = jnp.clip(jnp.exp(jax.random.uniform(key_of[2], (E_DEV,), jnp.float32, math.log(0.5), math.log(2.0))), 0.5, 2.0)
    disc_mask = draw_disc_mask(jax.random.fold_in(key_of[4], 71), 0)
    return dict(velocity=velocity, column_width=column_width, row_height=row_height, disc_mask=disc_mask)


gll_points = [-1.0, -0.8997579954114602, -0.6771862795107377, -0.3631174638261782, 0.0, 0.3631174638261782, 0.6771862795107377, 0.8997579954114602, 1.0]
gll_weights = [0.0277777777777778, 0.1654953615608055, 0.2745387125001617, 0.3464285109730463, 0.3715192743764172, 0.3464285109730463, 0.2745387125001617, 0.1654953615608055, 0.0277777777777778]
viscosity = 0.5
time_step = 0.02
thrust_coef = 4.0 / 3.0
highest = lax.Precision.HIGHEST

def node_tables():
    points = np.array(gll_points)
    identity = np.eye(9)
    differences = points[:, None] - points[None, :] + identity
    barycentric = 1.0 / np.prod(differences, axis=1)
    off_diagonal = barycentric[None, :] / barycentric[:, None] / differences * (1.0 - identity)
    derivative = off_diagonal - identity * off_diagonal.sum(axis=1)[:, None]
    return (jnp.asarray(derivative, dtype=jnp.float32), jnp.asarray(np.array(gll_weights), dtype=jnp.float32))

def spectral_tables(mode_count):
    planes = 3 * mode_count
    wave_index = jnp.arange(mode_count, dtype=jnp.int32)
    plane_index = jnp.arange(planes, dtype=jnp.int32)
    phase_index = wave_index[:, None] * plane_index[None, :] % planes
    angles = 2.0 * math.pi / planes * phase_index.astype(jnp.float32)
    cosine_table = jnp.cos(angles)
    sine_table = jnp.sin(angles)
    mode_weight = jnp.where(wave_index == 0, 1.0, 2.0).astype(jnp.float32)[:, None] / math.sqrt(mode_count)
    wave_number = 8.0 / mode_count * wave_index.astype(jnp.float32)[:, None]
    inverse = jnp.concatenate([mode_weight * cosine_table, -mode_weight * sine_table], axis=0)
    spanwise = jnp.concatenate([-wave_number * mode_weight * sine_table, -wave_number * mode_weight * cosine_table], axis=0)
    forward = math.sqrt(mode_count) / planes * jnp.concatenate([cosine_table, -sine_table], axis=0).T
    return (inverse, spanwise, forward)

def assemble(nodal_field):
    upper_layer = nodal_field[:, :, :, 8] + jnp.roll(nodal_field[:, :, :, 0], -1, axis=1)
    nodal_field = jnp.concatenate([jnp.roll(upper_layer, 1, axis=1)[:, :, :, None], nodal_field[:, :, :, 1:8], upper_layer[:, :, :, None]], axis=3)
    upper_layer = nodal_field[:, :, :, :, 8] + jnp.roll(nodal_field[:, :, :, :, 0], -1, axis=2)
    return jnp.concatenate([jnp.roll(upper_layer, 1, axis=2)[:, :, :, :, None], nodal_field[:, :, :, :, 1:8], upper_layer[:, :, :, :, None]], axis=4)

def apply_operator(nodal_field, derivative, quad_weights, ratio_x, ratio_y, jacobian, factor):
    grad_r = jnp.einsum('ij,pcejbl->pceibl', derivative, nodal_field, precision=highest)
    grad_s = jnp.einsum('ij,pceajl->pceail', derivative, nodal_field, precision=highest)
    flux_r = grad_r * quad_weights[None, None, None, :, :, None] * ratio_x[None, :, :, None, None, None]
    flux_s = grad_s * quad_weights[None, None, None, :, :, None] * ratio_y[None, :, :, None, None, None]
    stiffness = jnp.einsum('ji,pcejbl->pceibl', derivative, flux_r, precision=highest) + jnp.einsum('ji,pceajl->pceail', derivative, flux_s, precision=highest)
    masses = jacobian[None, :, :, None, None, None] * quad_weights[None, None, None, :, :, None] * nodal_field
    return assemble(factor * masses + viscosity * stiffness)

def weighted_sum(left_field, right_field, multiplicity):
    return lax.optimization_barrier(jnp.sum(left_field * right_field * multiplicity[None, None, None, :, :, None], axis=(1, 2, 3, 4)))

def reference(velocity, column_width, row_height, disc_mask):
    derivative, weights = node_tables()
    quad_weights = weights[:, None] * weights[None, :]
    node_index = jnp.arange(9)
    edge_count = jnp.where((node_index == 0) | (node_index == 8), 2.0, 1.0).astype(jnp.float32)
    multiplicity = 1.0 / (edge_count[:, None] * edge_count[None, :])
    planes = 3 * MODES
    inverse, spanwise, forward = spectral_tables(MODES)
    nodal_field = velocity.reshape(3, COLS, E_DEV, 9, 9, 2 * MODES)
    wavenumber = 8.0 / MODES * jnp.arange(MODES).astype(jnp.float32)
    plane_index = jnp.arange(planes)
    in_disc = ((plane_index >= 3 * planes // 8) & (plane_index < 5 * planes // 8)).astype(jnp.float32)
    disc_planes = 5 * planes // 8 - 3 * planes // 8
    disc_float = disc_mask.astype(jnp.float32).reshape(COLS, E_DEV)

    def column_tendency(inputs):
        column, col_width, disc_rows = inputs
        values = jnp.einsum('peabl,lq->peabq', column, inverse, precision=highest)
        along_z = jnp.einsum('peabl,lq->peabq', column, spanwise, precision=highest)
        along_x = 2.0 / col_width * jnp.einsum('ij,pejbq->peibq', derivative, values, precision=highest)
        along_y = (2.0 / row_height)[None, :, None, None, None] * jnp.einsum('ij,peajq->peaiq', derivative, values, precision=highest)
        advection = values[0][None] * along_x + values[1][None] * along_y + values[2][None] * along_z
        jacobian = col_width * row_height / 4.0
        node_weight = (disc_rows * jacobian)[:, None, None] * quad_weights[None]
        disc_total = jnp.sum(node_weight[:, :, :, None] * values[0] * values[0] * in_disc)
        disc_area = disc_planes * col_width * jnp.sum(disc_rows * row_height)
        pressure = disc_total / disc_area
        thrust = -(0.5 * thrust_coef * ORDER) * pressure / col_width * disc_rows[:, None, None, None] * in_disc
        tendency = jnp.concatenate([(thrust - advection[0])[None], -advection[1:]], axis=0)
        return jnp.einsum('peabq,ql->peabl', tendency, forward, precision=highest)
    columns = jnp.moveaxis(nodal_field, 1, 0)
    tendencies = lax.map(column_tendency, (columns, column_width, disc_float))
    tendency = jnp.moveaxis(tendencies, 0, 1)
    u_star = nodal_field + time_step * tendency
    jacobian = column_width[:, None] * row_height[None, :] / 4.0
    ratio_x = row_height[None, :] / column_width[:, None]
    ratio_y = column_width[:, None] / row_height[None, :]
    single = 1.0 / time_step + viscosity * wavenumber * wavenumber
    factor = jnp.concatenate([single, single])
    right_side = assemble(jacobian[None, :, :, None, None, None] * quad_weights[None, None, None, :, :, None] * u_star) / time_step
    residual = right_side
    direction = right_side
    solution = jnp.zeros_like(right_side)
    norm_now = weighted_sum(residual, residual, multiplicity)
    for iteration in range(ITERS):
        image_field = apply_operator(direction, derivative, quad_weights, ratio_x, ratio_y, jacobian, factor)
        step_size = (norm_now / weighted_sum(direction, image_field, multiplicity))[:, None, None, None, None, :]
        solution = solution + step_size * direction
        residual = residual - step_size * image_field
        if iteration + 1 < ITERS:
            norm_next = weighted_sum(residual, residual, multiplicity)
            direction = residual + (norm_next / norm_now)[:, None, None, None, None, :] * direction
            norm_now = norm_next
    return solution.reshape(3, NODES, 2, MODES)
```

```python
import math

import jax
import jax.numpy as jnp
import numpy as np
from jax import lax
from jax.experimental import pallas as pl
from jax.experimental.pallas import tpu as pltpu
from jax.sharding import PartitionSpec as P

ORDER = 8
NPT = 9
N2 = 81
PAD = 88
ROWS = 248

gll_points = [
    -1.0,
    -0.8997579954114602,
    -0.6771862795107377,
    -0.3631174638261782,
    0.0,
    0.3631174638261782,
    0.6771862795107377,
    0.8997579954114602,
    1.0,
]
gll_weights = [
    0.0277777777777778,
    0.1654953615608055,
    0.2745387125001617,
    0.3464285109730463,
    0.3715192743764172,
    0.3464285109730463,
    0.2745387125001617,
    0.1654953615608055,
    0.0277777777777778,
]
viscosity = 0.5
time_step = 0.02
thrust_coef = 4.0 / 3.0
f32 = jnp.float32
bf16 = jnp.bfloat16


def derivative_matrix():
    points = np.array(gll_points)
    identity = np.eye(9)
    differences = points[:, None] - points[None, :] + identity
    barycentric = 1.0 / np.prod(differences, axis=1)
    off_diagonal = barycentric[None, :] / barycentric[:, None] / differences * (1.0 - identity)
    return off_diagonal - identity * off_diagonal.sum(axis=1)[:, None]


def split_host(table):
    import ml_dtypes

    high = table.astype(np.float32).astype(ml_dtypes.bfloat16)
    low = (table - high.astype(np.float64)).astype(np.float32).astype(ml_dtypes.bfloat16)
    return jnp.asarray(high), jnp.asarray(low)


def split_xla(table):
    high = lax.reduce_precision(table, 8, 7)
    return high.astype(bf16), (table - high).astype(bf16)


def split(x):
    high = x.astype(bf16)
    return high, (x - high.astype(f32)).astype(bf16)


def dot(a, b):
    return jnp.dot(a, b, preferred_element_type=f32)


def dot_nt(a, b):
    return lax.dot_general(a, b, (((1,), (1,)), ((), ())), preferred_element_type=f32)


def dot3(a, b, d=dot):
    return d(a[0], b[0]) + d(a[0], b[1]) + d(a[1], b[0])


def physical_kernel(
    groups, modes, tile, planes, scale_ref, x_ref, chi, clo, shi, slo, ghi, glo, wk, w2,
    out_ref, xr, xi, rh, rl, ih, il, col0, acc_re, acc_im, press,
):
    q = pl.program_id(0)
    half = planes // 2

    @pl.when(q == 0)
    def _():
        xr[...] = jnp.zeros_like(xr)
        xi[...] = jnp.zeros_like(xi)
        for g in range(groups):
            lanes = slice(g * modes, (g + 1) * modes)
            cw = wk[0:1, lanes]
            ck = wk[1:2, lanes]
            for i in range(3):
                re = x_ref[g, 0, N2 * i : N2 * i + N2, :]
                im = x_ref[g, 1, N2 * i : N2 * i + N2, :]
                at = slice(PAD * i, PAD * i + N2)
                zt = slice(3 * PAD + PAD * i, 3 * PAD + PAD * i + N2)
                xr[at, lanes] = cw * re
                xi[at, lanes] = cw * im
                xr[zt, lanes] = -ck * im
                xi[zt, lanes] = ck * re
        full = xr[...]
        rh[...], rl[...] = split(full)
        ih[...], il[...] = split(xi[...])
        col0[...] = jnp.broadcast_to(
            jnp.sum(full * wk[2:3, :], axis=1, keepdims=True), col0.shape
        )
        acc_re[...] = jnp.zeros_like(acc_re)
        acc_im[...] = jnp.zeros_like(acc_im)
        press[...] = jnp.zeros_like(press)

    ctab = (chi[...], clo[...])
    stab = (shi[...], slo[...])
    cpart = dot3((rh[...], rl[...]), ctab)
    spart = dot3((ih[...], il[...]), stab)
    lane = lax.broadcasted_iota(jnp.int32, (1, tile), 1) + q * tile
    first = lane == 0
    side_a = cpart - spart
    side_b = jnp.where(first, col0[:, 0:1], cpart + spart)
    plane_b = jnp.where(first, half, planes - lane)
    grad = (ghi[...], glo[...])
    tend = []
    total = jnp.zeros((PAD, tile), f32)
    for side, plane in ((side_a, lane), (side_b, plane_b)):
        inside = ((plane >= 3 * planes // 8) & (plane < 5 * planes // 8)).astype(f32)
        u = [side[PAD * i : PAD * i + PAD] for i in range(3)]
        z = [side[3 * PAD + PAD * i : 4 * PAD + PAD * i] for i in range(3)]
        ux = u[0] * scale_ref[0]
        uy = u[1] * scale_ref[1]
        total = total + u[0] * u[0] * inside
        parts = []
        for i in range(3):
            g = dot3(grad, split(u[i]))
            parts.append(-(ux * g[:PAD] + uy * g[PAD:] + u[2] * z[i]))
        tend.append(jnp.concatenate(parts, axis=0))
    press[...] += total * w2[...]
    plus = split(tend[0] + tend[1])
    minus = split(tend[0] - tend[1])
    acc_re[...] += dot3(plus, ctab, dot_nt)
    acc_im[...] -= dot3(minus, stab, dot_nt)

    @pl.when(q == 0)
    def _():
        acc_re[...] += tend[1][:, 0:1] * (wk[2:3, :] - 1.0)

    @pl.when(q == pl.num_programs(0) - 1)
    def _():
        coef = math.sqrt(groups * modes) / planes
        whole = jnp.sum(jnp.sum(press[...], axis=1, keepdims=True), axis=0, keepdims=True)
        tail = jnp.broadcast_to(whole, (ROWS - 3 * N2, modes))
        for g in range(groups):
            lanes = slice(g * modes, (g + 1) * modes)
            for part, acc in ((0, acc_re), (1, acc_im)):
                for i in range(3):
                    out_ref[g, part, N2 * i : N2 * i + N2, :] = (
                        coef * acc[PAD * i : PAD * i + N2, lanes]
                    )
                out_ref[g, part, 3 * N2 : ROWS, :] = tail


def physical(received, scales, tables, grads, wk, w2):
    groups, _, _, modes = received.shape
    count = groups * modes
    planes = 3 * count
    half = planes // 2
    tile = 256 if half % 256 == 0 else half
    table_spec = pl.BlockSpec((count, tile), lambda q: (0, q))
    whole = lambda a: pl.BlockSpec(a.shape, lambda q: (0,) * a.ndim)
    body = lambda *refs: physical_kernel(groups, modes, tile, planes, *refs)
    flops = 3 * 2 * (6 * PAD + 3 * PAD) * count * planes
    return pl.pallas_call(
        body,
        grid=(half // tile,),
        out_shape=jax.ShapeDtypeStruct(received.shape, f32),
        in_specs=[pl.BlockSpec(memory_space=pltpu.SMEM), whole(received)]
        + [table_spec] * 4
        + [whole(grads[0]), whole(grads[1]), whole(wk), whole(w2)],
        out_specs=whole(received),
        scratch_shapes=[
            pltpu.VMEM((6 * PAD, count), f32),
            pltpu.VMEM((6 * PAD, count), f32),
            pltpu.VMEM((6 * PAD, count), bf16),
            pltpu.VMEM((6 * PAD, count), bf16),
            pltpu.VMEM((6 * PAD, count), bf16),
            pltpu.VMEM((6 * PAD, count), bf16),
            pltpu.VMEM((6 * PAD, 128), f32),
            pltpu.VMEM((3 * PAD, count), f32),
            pltpu.VMEM((3 * PAD, count), f32),
            pltpu.VMEM((PAD, tile), f32),
        ],
        cost_estimate=pl.CostEstimate(
            flops=flops, bytes_accessed=8 * count * half, transcendentals=0
        ),
        compiler_params=pltpu.CompilerParams(vmem_limit_bytes=48 << 20),
    )(scales, received, *tables, *grads, wk, w2)


def stiffness_line():
    d = derivative_matrix()
    w = np.array(gll_weights)
    k = d.T @ (w[:, None] * d)
    even = np.zeros((5, 5))
    odd = np.zeros((4, 4))
    for i in range(5):
        for j in range(5):
            even[i, j] = k[i, j] if j == 4 else 0.5 * (k[i, j] + k[i, 8 - j])
    for i in range(4):
        for j in range(4):
            odd[i, j] = 0.5 * (k[i, j] - k[i, 8 - j])
    return even, odd


def line_product(v, even, odd):
    s = [v[j] + v[8 - j] for j in range(4)] + [v[4]]
    t = [v[j] - v[8 - j] for j in range(4)]
    ev = [sum(float(even[i, j]) * s[j] for j in range(5)) for i in range(5)]
    od = [sum(float(odd[i, j]) * t[j] for j in range(4)) for i in range(4)]
    return [ev[i] + od[i] for i in range(4)] + [ev[4]] + [ev[i] - od[i] for i in range(3, -1, -1)]


def cg_kernel(
    chunks, groups, elems, modes, peers,
    mf_ref, rx_ref, ry_ref, jw_ref, cw_ref, th_ref, tk_ref, *refs,
):
    vel = refs[:chunks]
    ret = refs[chunks : 2 * chunks]
    out_ref = refs[2 * chunks]
    (r, qb, from_left, from_right, dots, gathered, coef, fs, fr, ds, dr) = refs[2 * chunks + 1 :]
    me = lax.axis_index("elem")
    face = NPT * elems
    w = gll_weights
    even, odd = stiffness_line()
    mult = [0.5] + [1.0] * 7 + [0.5]

    barrier = pltpu.get_barrier_semaphore()
    for k in range(1, peers):
        pl.semaphore_signal(
            barrier, inc=1, device_id={"elem": lax.rem(me + k, peers)},
            device_id_type=pl.DeviceIdType.MESH,
        )

    pressure = jnp.zeros((1, modes), f32)
    for e in range(elems):
        pressure = pressure + cw_ref[e : e + 1, :] * ret[e % chunks][
            e // chunks, 0, 3 * N2 : 3 * N2 + 1, :
        ]
    for e in range(elems):
        g, c = e // chunks, e % chunks
        for part in range(2):
            push = th_ref[e : e + 1, :] * pressure * tk_ref[part : part + 1, :]
            for i in range(3):
                rows = slice(N2 * i, N2 * i + N2)
                value = vel[c][g, part, rows, :] + time_step * ret[c][g, part, rows, :]
                if i == 0:
                    value = value + push
                r[2 * i + part, pl.ds(e, N2, stride=elems), :] = value

    def row(a, b):
        return pl.ds((a * NPT + b) * elems, elems)

    def joined(line):
        top = line[8] + pltpu.roll(line[0], elems - 1, 0)
        return [pltpu.roll(top, 1, 0)] + line[1:8] + [top]

    def masses(p, carry):
        jw = jw_ref[...]
        for a in range(NPT):
            line = [r[p, row(a, b), :] * (jw * (w[a] * w[b])) for b in range(NPT)]
            line = joined(line)
            for b in range(NPT):
                r[p, row(a, b), :] = line[b]
        return carry

    lax.fori_loop(0, 6, masses, 0)
    pl.semaphore_wait(barrier, peers - 1)

    right, left = lax.rem(me + 1, peers), lax.rem(me + peers - 1, peers)

    def face_copies(buffer, n):
        one = pltpu.make_async_remote_copy(
            src_ref=buffer.at[:, pl.ds(8 * face, face), :],
            dst_ref=from_left.at[n],
            send_sem=fs.at[2 * n],
            recv_sem=fr.at[2 * n],
            device_id={"elem": right},
            device_id_type=pl.DeviceIdType.MESH,
        )
        two = pltpu.make_async_remote_copy(
            src_ref=buffer.at[:, pl.ds(0, face), :],
            dst_ref=from_right.at[n],
            send_sem=fs.at[2 * n + 1],
            recv_sem=fr.at[2 * n + 1],
            device_id={"elem": left},
            device_id_type=pl.DeviceIdType.MESH,
        )
        return one, two

    def dot_copies(n):
        copies = []
        for k in range(1, peers):
            copies.append(
                pltpu.make_async_remote_copy(
                    src_ref=dots.at[n],
                    dst_ref=gathered.at[n, k - 1],
                    send_sem=ds.at[n, k - 1],
                    recv_sem=dr.at[n, k - 1],
                    device_id={"elem": lax.rem(me + k, peers)},
                    device_id_type=pl.DeviceIdType.MESH,
                )
            )
        return copies

    def add_faces(buffer, n):
        buffer[:, pl.ds(0, face), :] = buffer[:, pl.ds(0, face), :] + from_left[n]
        buffer[:, pl.ds(8 * face, face), :] = buffer[:, pl.ds(8 * face, face), :] + from_right[n]

    copies = face_copies(r, 0)
    for c in copies:
        c.start()
    for c in copies:
        c.wait()
    add_faces(r, 0)

    def squash(x):
        return jnp.sum(x, axis=0, keepdims=True)

    def apply_first(p, carry):
        mf, rx, ry = mf_ref[...], rx_ref[...], ry_ref[...]
        for b in range(NPT):
            v = [r[p, row(a, b), :] for a in range(NPT)]
            kx = line_product(v, even, odd)
            rxb = rx * w[b]
            mfb = mf * w[b]
            for a in range(NPT):
                qb[p, row(a, b), :] = (mfb * w[a]) * v[a] + rxb * kx[a]
        rr = jnp.zeros((elems, modes), f32)
        pq = jnp.zeros((elems, modes), f32)
        for a in range(NPT):
            v = [r[p, row(a, b), :] for b in range(NPT)]
            ky = line_product(v, even, odd)
            rya = ry * w[a]
            line = [qb[p, row(a, b), :] + rya * ky[b] for b in range(NPT)]
            for b in range(NPT):
                rr = rr + (mult[a] * mult[b]) * (v[b] * v[b])
                pq = pq + v[b] * line[b]
            line = joined(line)
            for b in range(NPT):
                qb[p, row(a, b), :] = line[b]
        dots[0, pl.ds(p, 1), :] = squash(rr)
        dots[0, pl.ds(8 + p, 1), :] = squash(pq)
        return carry

    dots[...] = jnp.zeros_like(dots)
    lax.fori_loop(0, 6, apply_first, 0)
    faces = face_copies(qb, 1)
    sums = dot_copies(0)
    for c in faces + tuple(sums):
        c.start()
    for c in sums:
        c.wait()
    total = dots[0]
    for k in range(peers - 1):
        total = total + gathered[0, k]
    norm = total[0:8]
    alpha = norm / total[8:16]
    coef[0] = alpha
    for c in faces:
        c.wait()
    add_faces(qb, 1)

    def apply_second(p, carry):
        mf, rx, ry = mf_ref[...], rx_ref[...], ry_ref[...]
        al = coef[0, pl.ds(p, 1), :]
        rz = jnp.zeros((elems, modes), f32)
        rr = jnp.zeros((elems, modes), f32)
        for b in range(NPT):
            v = [r[p, row(a, b), :] - al * qb[p, row(a, b), :] for a in range(NPT)]
            kx = line_product(v, even, odd)
            one = jnp.zeros((elems, modes), f32)
            two = jnp.zeros((elems, modes), f32)
            for a in range(NPT):
                qb[p, row(a, b), :] = v[a]
                square = v[a] * v[a]
                one = one + v[a] * kx[a]
                two = two + w[a] * square
                rr = rr + (mult[a] * mult[b]) * square
            rz = rz + w[b] * (rx * one + mf * two)
        for a in range(NPT):
            v = [qb[p, row(a, b), :] for b in range(NPT)]
            ky = line_product(v, even, odd)
            one = jnp.zeros((elems, modes), f32)
            for b in range(NPT):
                one = one + v[b] * ky[b]
            rz = rz + (w[a] * ry) * one
        dots[1, pl.ds(p, 1), :] = squash(rr)
        dots[1, pl.ds(8 + p, 1), :] = squash(rz)
        return carry

    lax.fori_loop(0, 6, apply_second, 0)
    sums = dot_copies(1)
    for c in sums:
        c.start()
    for c in sums:
        c.wait()
    later = dots[1]
    for k in range(peers - 1):
        later = later + gathered[1, k]
    following = later[0:8]
    beta = following / norm
    second = following / (later[8:16] - beta * following / alpha)
    coef[0] = alpha + second * beta
    coef[1] = second

    def finish(p, carry):
        first = coef[0, pl.ds(p, 1), :]
        last = coef[1, pl.ds(p, 1), :]
        r[p] = first * r[p] + last * qb[p]
        return carry

    lax.fori_loop(0, 6, finish, 0)
    for i in range(3):
        for part in range(2):
            for e in range(elems):
                out_ref[i, part, e * N2 : e * N2 + N2, :] = r[
                    2 * i + part, pl.ds(e, N2, stride=elems), :
                ]


def conjugate_gradients(vels, rets, small):
    chunks = len(vels)
    groups, _, _, modes = vels[0].shape
    elems = groups * chunks
    peers = lax.axis_size("elem")
    body = lambda *refs: cg_kernel(chunks, groups, elems, modes, peers, *refs)
    vm = pl.BlockSpec(memory_space=pltpu.VMEM)
    return pl.pallas_call(
        body,
        out_shape=jax.ShapeDtypeStruct((3, 2, elems * N2, modes), f32),
        in_specs=[vm] * (len(small) + 2 * chunks),
        out_specs=vm,
        scratch_shapes=[
            pltpu.VMEM((6, N2 * elems, modes), f32),
            pltpu.VMEM((6, N2 * elems, modes), f32),
            pltpu.VMEM((2, 6, NPT * elems, modes), f32),
            pltpu.VMEM((2, 6, NPT * elems, modes), f32),
            pltpu.VMEM((2, 16, modes), f32),
            pltpu.VMEM((2, peers - 1, 16, modes), f32),
            pltpu.VMEM((2, 8, modes), f32),
            pltpu.SemaphoreType.DMA((4,)),
            pltpu.SemaphoreType.DMA((4,)),
            pltpu.SemaphoreType.DMA((2, peers - 1)),
            pltpu.SemaphoreType.DMA((2, peers - 1)),
        ],
        compiler_params=pltpu.CompilerParams(
            collective_id=0, has_side_effects=True, vmem_limit_bytes=48 << 20
        ),
    )(*small, *vels, *rets)


def on_device(velocity, column_width, row_height, disc_mask):
    groups = lax.axis_size("mode")
    modes = velocity.shape[3]
    count = groups * modes
    planes = 3 * count
    half = planes // 2
    elems = velocity.shape[1] // N2
    chunks = elems // groups
    mine = lax.axis_index("mode")
    hx = column_width[0]

    shaped = velocity.reshape(3, groups, chunks, N2, 2, modes)
    vels = []
    for c in range(chunks):
        piece = jnp.transpose(shaped[:, :, c], (1, 3, 0, 2, 4)).reshape(groups, 2, 3 * N2, modes)
        vels.append(jnp.pad(piece, ((0, 0), (0, 0), (0, ROWS - 3 * N2), (0, 0))))
    received = [lax.all_to_all(v, "mode", 0, 0, tiled=True) for v in vels]

    k = jnp.arange(count, dtype=jnp.int32)
    j = jnp.arange(half, dtype=jnp.int32)
    phase = k[:, None] * j[None, :] % planes
    angles = 2.0 * math.pi / planes * phase.astype(f32)
    tables = split_xla(jnp.cos(angles)) + split_xla(jnp.sin(angles))

    derivative = derivative_matrix()
    stacked = np.zeros((2 * PAD, PAD))
    stacked[:N2, :N2] = np.kron(derivative, np.eye(9))
    stacked[PAD : PAD + N2, :N2] = np.kron(np.eye(9), derivative)
    grads = split_host(stacked)
    host_k = np.arange(count)
    weight = np.where(host_k == 0, 1.0, 2.0) / math.sqrt(count)
    wk = np.zeros((8, count), np.float32)
    wk[0] = weight
    wk[1] = weight * (8.0 / count) * host_k
    wk[2] = 1.0 - 2.0 * (host_k % 2)
    wk = jnp.asarray(wk)
    w = np.array(gll_weights)
    tile = 256 if half % 256 == 0 else half
    w2 = np.zeros((PAD, 1), np.float32)
    w2[:N2, 0] = (w[:, None] * w[None, :]).reshape(-1)
    w2 = jnp.asarray(np.broadcast_to(w2, (PAD, tile)))

    rets = []
    for c in range(chunks):
        hy = lax.dynamic_index_in_dim(row_height, mine * chunks + c, keepdims=False)
        scales = jnp.stack([2.0 / hx, 2.0 / hy])
        spectral = physical(received[c], scales, tables, grads, wk, w2)
        rets.append(lax.all_to_all(spectral, "mode", 0, 0, tiled=True))

    disc = disc_mask.astype(f32)
    jacobian = hx * row_height / 4.0
    disc_planes = 5 * planes // 8 - 3 * planes // 8
    area = disc_planes * hx * jnp.sum(disc * row_height)
    spread = lambda x: jnp.broadcast_to(x[:, None], (elems, modes))
    local_k = (mine * modes + jnp.arange(modes, dtype=jnp.int32)).astype(f32)
    kz = 8.0 / count * local_k
    factor = 1.0 / time_step + viscosity * kz * kz
    in_planes = np.arange(3 * planes // 8, 5 * planes // 8)
    arg = 2.0 * np.pi * ((host_k[:, None] * in_planes[None, :]) % planes) / planes
    profile = math.sqrt(count) / planes * np.stack([np.cos(arg).sum(1), -np.sin(arg).sum(1)])
    profile = jnp.asarray(profile.astype(np.float32)).reshape(2, groups, modes)
    small = (
        jacobian[:, None] * factor[None, :],
        spread(viscosity * row_height / hx),
        spread(viscosity * hx / row_height),
        spread(jacobian / time_step),
        spread(disc * jacobian),
        spread(-(0.5 * thrust_coef * ORDER * time_step) / hx * disc / area),
        lax.dynamic_index_in_dim(profile, mine, axis=1, keepdims=False),
    )
    result = conjugate_gradients(vels, rets, small)
    result = result.reshape(3, 2, elems * N2, modes)
    return jnp.transpose(result, (0, 2, 1, 3))


def solution(mesh):
    return jax.shard_map(
        on_device,
        mesh=mesh,
        in_specs=(P(None, "elem", None, "mode"), P("elem"), P(), P("elem")),
        out_specs=P(None, "elem", None, "mode"),
        check_vma=False,
    )
```

```python
import math

import jax
import jax.numpy as jnp
import numpy as np
from jax import lax
from jax.experimental import pallas as pl
from jax.experimental.pallas import tpu as pltpu
from jax.sharding import PartitionSpec as P

ORDER = 8
NPT = 9
N2 = 81
PAD = 88
ROWS = 248

gll_points = [
    -1.0,
    -0.8997579954114602,
    -0.6771862795107377,
    -0.3631174638261782,
    0.0,
    0.3631174638261782,
    0.6771862795107377,
    0.8997579954114602,
    1.0,
]
gll_weights = [
    0.0277777777777778,
    0.1654953615608055,
    0.2745387125001617,
    0.3464285109730463,
    0.3715192743764172,
    0.3464285109730463,
    0.2745387125001617,
    0.1654953615608055,
    0.0277777777777778,
]
viscosity = 0.5
time_step = 0.02
thrust_coef = 4.0 / 3.0
f32 = jnp.float32
bf16 = jnp.bfloat16


def derivative_matrix():
    points = np.array(gll_points)
    identity = np.eye(9)
    differences = points[:, None] - points[None, :] + identity
    barycentric = 1.0 / np.prod(differences, axis=1)
    off_diagonal = barycentric[None, :] / barycentric[:, None] / differences * (1.0 - identity)
    return off_diagonal - identity * off_diagonal.sum(axis=1)[:, None]


def split_host(table):
    import ml_dtypes

    high = table.astype(np.float32).astype(ml_dtypes.bfloat16)
    low = (table - high.astype(np.float64)).astype(np.float32).astype(ml_dtypes.bfloat16)
    return jnp.asarray(high), jnp.asarray(low)


def split(x):
    high = x.astype(bf16)
    return high, (x - high.astype(f32)).astype(bf16)


def dot(a, b):
    return jnp.dot(a, b, preferred_element_type=f32)


def dot_nt(a, b):
    return lax.dot_general(a, b, (((1,), (1,)), ((), ())), preferred_element_type=f32)


def dot3(a, b, d=dot):
    return d(a[0], b[0]) + d(a[0], b[1]) + d(a[1], b[0])


def advect_chunk(groups, modes, tile, planes, scales, x, spec, small, tabs, scratch):
    ghi, glo, wk, w2 = small
    ch, cl, sh, sl = tabs
    xr, xi, rh, rl, ih, il, col0, acc_re, acc_im, press = scratch
    half = planes // 2
    for g in range(groups):
        lanes = slice(g * modes, (g + 1) * modes)
        cw = wk[0:1, lanes]
        ck = wk[1:2, lanes]
        for i in range(3):
            re = x[g, 0, N2 * i : N2 * i + N2, :]
            im = x[g, 1, N2 * i : N2 * i + N2, :]
            at = slice(PAD * i, PAD * i + N2)
            zt = slice(3 * PAD + PAD * i, 3 * PAD + PAD * i + N2)
            xr[at, lanes] = cw * re
            xi[at, lanes] = cw * im
            xr[zt, lanes] = -ck * im
            xi[zt, lanes] = ck * re
    full = xr[...]
    rh[...], rl[...] = split(full)
    ih[...], il[...] = split(xi[...])
    col0[...] = jnp.broadcast_to(jnp.sum(full * wk[2:3, :], axis=1, keepdims=True), col0.shape)
    acc_re[...] = jnp.zeros_like(acc_re)
    acc_im[...] = jnp.zeros_like(acc_im)
    press[...] = jnp.zeros_like(press)

    def step(q, carry):
        ctab = (ch[q], cl[q])
        stab = (sh[q], sl[q])
        cpart = dot3((rh[...], rl[...]), ctab)
        spart = dot3((ih[...], il[...]), stab)
        lane = lax.broadcasted_iota(jnp.int32, (1, tile), 1) + q * tile
        first = lane == 0
        side_a = cpart - spart
        side_b = jnp.where(first, col0[:, 0:1], cpart + spart)
        plane_b = jnp.where(first, half, planes - lane)
        grad = (ghi[...], glo[...])
        tend = []
        total = jnp.zeros((PAD, tile), f32)
        for side, plane in ((side_a, lane), (side_b, plane_b)):
            inside = ((plane >= 3 * planes // 8) & (plane < 5 * planes // 8)).astype(f32)
            u = [side[PAD * i : PAD * i + PAD] for i in range(3)]
            z = [side[3 * PAD + PAD * i : 4 * PAD + PAD * i] for i in range(3)]
            ux = u[0] * scales[0]
            uy = u[1] * scales[1]
            total = total + u[0] * u[0] * inside
            parts = []
            for i in range(3):
                g = dot3(grad, split(u[i]))
                parts.append(-(ux * g[:PAD] + uy * g[PAD:] + u[2] * z[i]))
            tend.append(jnp.concatenate(parts, axis=0))
        press[...] += total * w2[...]
        plus = split(tend[0] + tend[1])
        minus = split(tend[0] - tend[1])
        acc_re[...] += dot3(plus, ctab, dot_nt)
        acc_im[...] -= dot3(minus, stab, dot_nt)

        @pl.when(q == 0)
        def _():
            acc_re[...] += tend[1][:, 0:1] * (wk[2:3, :] - 1.0)

        return carry

    lax.fori_loop(0, half // tile, step, 0)
    coef = math.sqrt(groups * modes) / planes
    whole = jnp.sum(jnp.sum(press[...], axis=1, keepdims=True), axis=0, keepdims=True)
    tail = jnp.broadcast_to(whole, (ROWS - 3 * N2, modes))
    for g in range(groups):
        lanes = slice(g * modes, (g + 1) * modes)
        for part, acc in ((0, acc_re), (1, acc_im)):
            for i in range(3):
                spec[g, part, N2 * i : N2 * i + N2, :] = (
                    coef * acc[PAD * i : PAD * i + N2, lanes]
                )
            spec[g, part, 3 * N2 : ROWS, :] = tail


def partners(me, groups):
    if groups == 4:
        return [lax.rem(me + 2, 4), 3 - me, me + 1 - 2 * lax.rem(me, 2)]
    return [lax.rem(me + k, groups) for k in range(1, groups)]


def stiffness_line():
    d = derivative_matrix()
    w = np.array(gll_weights)
    k = d.T @ (w[:, None] * d)
    even = np.zeros((5, 5))
    odd = np.zeros((4, 4))
    for i in range(5):
        for j in range(5):
            even[i, j] = k[i, j] if j == 4 else 0.5 * (k[i, j] + k[i, 8 - j])
    for i in range(4):
        for j in range(4):
            odd[i, j] = 0.5 * (k[i, j] - k[i, 8 - j])
    return even, odd


def line_product(v, even, odd):
    s = [v[j] + v[8 - j] for j in range(4)] + [v[4]]
    t = [v[j] - v[8 - j] for j in range(4)]
    ev = [sum(float(even[i, j]) * s[j] for j in range(5)) for i in range(5)]
    od = [sum(float(odd[i, j]) * t[j] for j in range(4)) for i in range(4)]
    return [ev[i] + od[i] for i in range(4)] + [ev[4]] + [ev[i] - od[i] for i in range(3, -1, -1)]


def window_kernel(
    chunks, groups, elems, modes, peers, tile,
    scale_ref, mf_ref, rx_ref, ry_ref, jw_ref, cw_ref, th_ref, tk_ref,
    cbase, sbase, rot, ghi, glo, wk, w2, *refs,
):
    vel = refs[:chunks]
    out_ref = refs[chunks]
    (
        r, qb, from_left, from_right, dots, gathered, coef, fs, fr, ds, dr,
        recv, spec, ret, ch, cl, sh, sl, ms, mr, *scratch,
    ) = refs[chunks + 1 :]
    me = lax.axis_index("elem")
    slot = lax.axis_index("mode")
    planes = 3 * groups * modes
    face = NPT * elems
    w = gll_weights
    even, odd = stiffness_line()
    mult = [0.5] + [1.0] * 7 + [0.5]
    others = partners(slot, groups)

    barrier = pltpu.get_barrier_semaphore()
    for k in range(1, peers):
        pl.semaphore_signal(
            barrier, inc=1, device_id={"elem": lax.rem(me + k, peers)},
            device_id_type=pl.DeviceIdType.MESH,
        )
    for other in others:
        pl.semaphore_signal(
            barrier, inc=1, device_id={"mode": other}, device_id_type=pl.DeviceIdType.MESH
        )
    pl.semaphore_wait(barrier, peers - 1 + groups - 1)

    def exchange(source, target, n):
        return [
            pltpu.make_async_remote_copy(
                src_ref=source.at[other],
                dst_ref=target.at[slot],
                send_sem=ms.at[n, k],
                recv_sem=mr.at[n, k],
                device_id={"mode": other},
                device_id_type=pl.DeviceIdType.MESH,
            )
            for k, other in enumerate(others)
        ]

    outward = [exchange(vel[c], recv.at[c], c) for c in range(chunks)]
    for copies in outward:
        for copy in copies:
            copy.start()
    for c in range(chunks):
        recv[c, slot] = vel[c][slot]
    xr, xi = scratch[0], scratch[1]
    xr[...] = jnp.zeros_like(xr)
    xi[...] = jnp.zeros_like(xi)
    cos0, sin0 = cbase[...], sbase[...]
    for q in range(planes // 2 // tile):
        cq, sq = rot[:, 2 * q : 2 * q + 1], rot[:, 2 * q + 1 : 2 * q + 2]
        ch[q], cl[q] = split(cos0 * cq - sin0 * sq)
        sh[q], sl[q] = split(sin0 * cq + cos0 * sq)

    inward = []
    for c in range(chunks):
        for copy in outward[c]:
            copy.wait()
        scales = (scale_ref[c, 0], scale_ref[c, 1])
        advect_chunk(
            groups, modes, tile, planes, scales, recv.at[c], spec.at[c],
            (ghi, glo, wk, w2), (ch, cl, sh, sl), scratch,
        )
        copies = exchange(spec.at[c], ret.at[c], chunks + c)
        for copy in copies:
            copy.start()
        ret[c, slot] = spec[c, slot]
        inward.append(copies)

    for c in range(chunks):
        for copy in inward[c]:
            copy.wait()
        for g in range(groups):
            for part in range(2):
                for i in range(3):
                    rows = slice(N2 * i, N2 * i + N2)
                    value = vel[c][g, part, rows, :] + time_step * ret[c, g, part, rows, :]
                    r[2 * i + part, pl.ds(g * chunks + c, N2, stride=elems), :] = value
    pressure = jnp.zeros((1, modes), f32)
    for e in range(elems):
        pressure = pressure + cw_ref[e : e + 1, :] * ret[
            e % chunks, e // chunks, 0, 3 * N2 : 3 * N2 + 1, :
        ]
    push_all = th_ref[...] * pressure

    def row(a, b):
        return pl.ds((a * NPT + b) * elems, elems)

    def joined(line):
        top = line[8] + pltpu.roll(line[0], elems - 1, 0)
        return [pltpu.roll(top, 1, 0)] + line[1:8] + [top]

    def masses(p, carry):
        jw = jw_ref[...]
        push = push_all * tk_ref[pl.ds(p, 1), :]
        for a in range(NPT):
            line = [(r[p, row(a, b), :] + push) * (jw * (w[a] * w[b])) for b in range(NPT)]
            line = joined(line)
            for b in range(NPT):
                r[p, row(a, b), :] = line[b]
        return carry

    lax.fori_loop(0, 6, masses, 0)

    right, left = lax.rem(me + 1, peers), lax.rem(me + peers - 1, peers)

    def face_copies(buffer, n):
        one = pltpu.make_async_remote_copy(
            src_ref=buffer.at[:, pl.ds(8 * face, face), :],
            dst_ref=from_left.at[n],
            send_sem=fs.at[2 * n],
            recv_sem=fr.at[2 * n],
            device_id={"elem": right},
            device_id_type=pl.DeviceIdType.MESH,
        )
        two = pltpu.make_async_remote_copy(
            src_ref=buffer.at[:, pl.ds(0, face), :],
            dst_ref=from_right.at[n],
            send_sem=fs.at[2 * n + 1],
            recv_sem=fr.at[2 * n + 1],
            device_id={"elem": left},
            device_id_type=pl.DeviceIdType.MESH,
        )
        return one, two

    def dot_copies(n):
        copies = []
        for k in range(1, peers):
            copies.append(
                pltpu.make_async_remote_copy(
                    src_ref=dots.at[n],
                    dst_ref=gathered.at[n, k - 1],
                    send_sem=ds.at[n, k - 1],
                    recv_sem=dr.at[n, k - 1],
                    device_id={"elem": lax.rem(me + k, peers)},
                    device_id_type=pl.DeviceIdType.MESH,
                )
            )
        return copies

    def add_faces(buffer, n):
        buffer[:, pl.ds(0, face), :] = buffer[:, pl.ds(0, face), :] + from_left[n]
        buffer[:, pl.ds(8 * face, face), :] = buffer[:, pl.ds(8 * face, face), :] + from_right[n]

    copies = face_copies(r, 0)
    for c in copies:
        c.start()
    for c in copies:
        c.wait()
    add_faces(r, 0)

    def squash(x):
        return jnp.sum(x, axis=0, keepdims=True)

    def apply_first(p, carry):
        mf, rx, ry = mf_ref[...], rx_ref[...], ry_ref[...]
        for b in range(NPT):
            v = [r[p, row(a, b), :] for a in range(NPT)]
            kx = line_product(v, even, odd)
            rxb = rx * w[b]
            mfb = mf * w[b]
            for a in range(NPT):
                qb[p, row(a, b), :] = (mfb * w[a]) * v[a] + rxb * kx[a]
        rr = jnp.zeros((elems, modes), f32)
        pq = jnp.zeros((elems, modes), f32)
        for a in range(NPT):
            v = [r[p, row(a, b), :] for b in range(NPT)]
            ky = line_product(v, even, odd)
            rya = ry * w[a]
            line = [qb[p, row(a, b), :] + rya * ky[b] for b in range(NPT)]
            for b in range(NPT):
                rr = rr + (mult[a] * mult[b]) * (v[b] * v[b])
                pq = pq + v[b] * line[b]
            line = joined(line)
            for b in range(NPT):
                qb[p, row(a, b), :] = line[b]
        dots[0, pl.ds(p, 1), :] = squash(rr)
        dots[0, pl.ds(8 + p, 1), :] = squash(pq)
        return carry

    dots[...] = jnp.zeros_like(dots)
    lax.fori_loop(0, 6, apply_first, 0)
    faces = face_copies(qb, 1)
    sums = dot_copies(0)
    for c in faces + tuple(sums):
        c.start()
    for c in sums:
        c.wait()
    total = dots[0]
    for k in range(peers - 1):
        total = total + gathered[0, k]
    norm = total[0:8]
    alpha = norm / total[8:16]
    coef[0] = alpha
    for c in faces:
        c.wait()
    add_faces(qb, 1)

    def apply_second(p, carry):
        mf, rx, ry = mf_ref[...], rx_ref[...], ry_ref[...]
        al = coef[0, pl.ds(p, 1), :]
        rz = jnp.zeros((elems, modes), f32)
        rr = jnp.zeros((elems, modes), f32)
        for b in range(NPT):
            v = [r[p, row(a, b), :] - al * qb[p, row(a, b), :] for a in range(NPT)]
            kx = line_product(v, even, odd)
            one = jnp.zeros((elems, modes), f32)
            two = jnp.zeros((elems, modes), f32)
            for a in range(NPT):
                qb[p, row(a, b), :] = v[a]
                square = v[a] * v[a]
                one = one + v[a] * kx[a]
                two = two + w[a] * square
                rr = rr + (mult[a] * mult[b]) * square
            rz = rz + w[b] * (rx * one + mf * two)
        for a in range(NPT):
            v = [qb[p, row(a, b), :] for b in range(NPT)]
            ky = line_product(v, even, odd)
            one = jnp.zeros((elems, modes), f32)
            for b in range(NPT):
                one = one + v[b] * ky[b]
            rz = rz + (w[a] * ry) * one
        dots[1, pl.ds(p, 1), :] = squash(rr)
        dots[1, pl.ds(8 + p, 1), :] = squash(rz)
        return carry

    lax.fori_loop(0, 6, apply_second, 0)
    sums = dot_copies(1)
    for c in sums:
        c.start()
    for c in sums:
        c.wait()
    later = dots[1]
    for k in range(peers - 1):
        later = later + gathered[1, k]
    following = later[0:8]
    beta = following / norm
    second = following / (later[8:16] - beta * following / alpha)
    coef[0] = alpha + second * beta
    coef[1] = second

    def finish(p, carry):
        first = coef[0, pl.ds(p, 1), :]
        last = coef[1, pl.ds(p, 1), :]
        r[p] = first * r[p] + last * qb[p]
        return carry

    lax.fori_loop(0, 6, finish, 0)
    for i in range(3):
        for part in range(2):
            for e in range(elems):
                out_ref[i, part, e * N2 : e * N2 + N2, :] = r[
                    2 * i + part, pl.ds(e, N2, stride=elems), :
                ]


def window(vels, scales, small, tables):
    chunks = len(vels)
    groups, _, _, modes = vels[0].shape
    elems = groups * chunks
    count = groups * modes
    half = 3 * count // 2
    tile = tables[0].shape[1]
    peers = lax.axis_size("elem")
    body = lambda *refs: window_kernel(chunks, groups, elems, modes, peers, tile, *refs)
    vm = pl.BlockSpec(memory_space=pltpu.VMEM)
    block = (chunks, groups, 2, ROWS, modes)
    table = pltpu.VMEM((half // tile, count, tile), bf16)
    return pl.pallas_call(
        body,
        out_shape=jax.ShapeDtypeStruct((3, 2, elems * N2, modes), f32),
        in_specs=[pl.BlockSpec(memory_space=pltpu.SMEM)]
        + [vm] * (len(small) + len(tables) + chunks),
        out_specs=vm,
        scratch_shapes=[
            pltpu.VMEM((6, N2 * elems, modes), f32),
            pltpu.VMEM((6, N2 * elems, modes), f32),
            pltpu.VMEM((2, 6, NPT * elems, modes), f32),
            pltpu.VMEM((2, 6, NPT * elems, modes), f32),
            pltpu.VMEM((2, 16, modes), f32),
            pltpu.VMEM((2, peers - 1, 16, modes), f32),
            pltpu.VMEM((2, 8, modes), f32),
            pltpu.SemaphoreType.DMA((4,)),
            pltpu.SemaphoreType.DMA((4,)),
            pltpu.SemaphoreType.DMA((2, peers - 1)),
            pltpu.SemaphoreType.DMA((2, peers - 1)),
            pltpu.VMEM(block, f32),
            pltpu.VMEM(block, f32),
            pltpu.VMEM(block, f32),
            table,
            table,
            table,
            table,
            pltpu.SemaphoreType.DMA((2 * chunks, groups - 1)),
            pltpu.SemaphoreType.DMA((2 * chunks, groups - 1)),
            pltpu.VMEM((6 * PAD, count), f32),
            pltpu.VMEM((6 * PAD, count), f32),
            pltpu.VMEM((6 * PAD, count), bf16),
            pltpu.VMEM((6 * PAD, count), bf16),
            pltpu.VMEM((6 * PAD, count), bf16),
            pltpu.VMEM((6 * PAD, count), bf16),
            pltpu.VMEM((6 * PAD, 128), f32),
            pltpu.VMEM((3 * PAD, count), f32),
            pltpu.VMEM((3 * PAD, count), f32),
            pltpu.VMEM((PAD, tile), f32),
        ],
        compiler_params=pltpu.CompilerParams(
            collective_id=0, has_side_effects=True, vmem_limit_bytes=56 << 20
        ),
    )(scales, *small, *tables, *vels)


def on_device(velocity, column_width, row_height, disc_mask):
    groups = lax.axis_size("mode")
    modes = velocity.shape[3]
    count = groups * modes
    planes = 3 * count
    half = planes // 2
    elems = velocity.shape[1] // N2
    chunks = elems // groups
    mine = lax.axis_index("mode")
    hx = column_width[0]

    shaped = velocity.reshape(3, groups, chunks, N2, 2, modes)
    vels = []
    for c in range(chunks):
        piece = jnp.transpose(shaped[:, :, c], (1, 3, 0, 2, 4)).reshape(groups, 2, 3 * N2, modes)
        vels.append(jnp.pad(piece, ((0, 0), (0, 0), (0, ROWS - 3 * N2), (0, 0))))
    derivative = derivative_matrix()
    stacked = np.zeros((2 * PAD, PAD))
    stacked[:N2, :N2] = np.kron(derivative, np.eye(9))
    stacked[PAD : PAD + N2, :N2] = np.kron(np.eye(9), derivative)
    grads = split_host(stacked)
    host_k = np.arange(count)
    weight = np.where(host_k == 0, 1.0, 2.0) / math.sqrt(count)
    wk = np.zeros((8, count), np.float32)
    wk[0] = weight
    wk[1] = weight * (8.0 / count) * host_k
    wk[2] = 1.0 - 2.0 * (host_k % 2)
    wk = jnp.asarray(wk)
    w = np.array(gll_weights)
    tile = 256 if half % 256 == 0 else half
    w2 = np.zeros((PAD, 1), np.float32)
    w2[:N2, 0] = (w[:, None] * w[None, :]).reshape(-1)
    w2 = jnp.asarray(np.broadcast_to(w2, (PAD, tile)))

    turn = 2.0 * np.pi / planes
    base = turn * (host_k[:, None] * np.arange(tile)[None, :] % planes)
    steps = turn * (host_k[:, None] * tile * np.arange(half // tile)[None, :] % planes)
    rotation = np.stack([np.cos(steps), np.sin(steps)], axis=2).reshape(count, -1)
    tables = tuple(jnp.asarray(t.astype(np.float32)) for t in (np.cos(base), np.sin(base), rotation))
    tables = tables + grads + (wk, w2)
    heights = lax.dynamic_slice_in_dim(row_height, mine * chunks, chunks)
    scales = jnp.stack([jnp.broadcast_to(2.0 / hx, (chunks,)), 2.0 / heights], axis=1)

    disc = disc_mask.astype(f32)
    jacobian = hx * row_height / 4.0
    disc_planes = 5 * planes // 8 - 3 * planes // 8
    area = disc_planes * hx * jnp.sum(disc * row_height)
    spread = lambda x: jnp.broadcast_to(x[:, None], (elems, modes))
    local_k = (mine * modes + jnp.arange(modes, dtype=jnp.int32)).astype(f32)
    kz = 8.0 / count * local_k
    factor = 1.0 / time_step + viscosity * kz * kz
    in_planes = np.arange(3 * planes // 8, 5 * planes // 8)
    arg = 2.0 * np.pi * ((host_k[:, None] * in_planes[None, :]) % planes) / planes
    profile = math.sqrt(count) / planes * np.stack([np.cos(arg).sum(1), -np.sin(arg).sum(1)])
    profile = np.concatenate([profile, np.zeros((6, count))])
    profile = jnp.asarray(profile.astype(np.float32)).reshape(8, groups, modes)
    small = (
        jacobian[:, None] * factor[None, :],
        spread(viscosity * row_height / hx),
        spread(viscosity * hx / row_height),
        spread(jacobian / time_step),
        spread(disc * jacobian),
        spread(-(0.5 * thrust_coef * ORDER * time_step) / hx * disc / area),
        lax.dynamic_index_in_dim(profile, mine, axis=1, keepdims=False),
    )
    result = window(vels, scales, small, tables)
    result = result.reshape(3, 2, elems * N2, modes)
    return jnp.transpose(result, (0, 2, 1, 3))


def solution(mesh):
    return jax.shard_map(
        on_device,
        mesh=mesh,
        in_specs=(P(None, "elem", None, "mode"), P("elem"), P(), P("elem")),
        out_specs=P(None, "elem", None, "mode"),
        check_vma=False,
    )
```

```python
import math

import jax
import jax.numpy as jnp
import numpy as np
from jax import lax
from jax.experimental import pallas as pl
from jax.experimental.pallas import tpu as pltpu
from jax.sharding import PartitionSpec as P

ORDER = 8
NPT = 9
N2 = 81
PAD = 88
ROWS = 248

gll_points = [
    -1.0,
    -0.8997579954114602,
    -0.6771862795107377,
    -0.3631174638261782,
    0.0,
    0.3631174638261782,
    0.6771862795107377,
    0.8997579954114602,
    1.0,
]
gll_weights = [
    0.0277777777777778,
    0.1654953615608055,
    0.2745387125001617,
    0.3464285109730463,
    0.3715192743764172,
    0.3464285109730463,
    0.2745387125001617,
    0.1654953615608055,
    0.0277777777777778,
]
viscosity = 0.5
time_step = 0.02
thrust_coef = 4.0 / 3.0
f32 = jnp.float32
bf16 = jnp.bfloat16


def derivative_matrix():
    points = np.array(gll_points)
    identity = np.eye(9)
    differences = points[:, None] - points[None, :] + identity
    barycentric = 1.0 / np.prod(differences, axis=1)
    off_diagonal = barycentric[None, :] / barycentric[:, None] / differences * (1.0 - identity)
    return off_diagonal - identity * off_diagonal.sum(axis=1)[:, None]


def split_host(table):
    import ml_dtypes

    high = table.astype(np.float32).astype(ml_dtypes.bfloat16)
    low = (table - high.astype(np.float64)).astype(np.float32).astype(ml_dtypes.bfloat16)
    return jnp.asarray(high), jnp.asarray(low)


def split(x):
    high = x.astype(bf16)
    return high, (x - high.astype(f32)).astype(bf16)


def dot(a, b):
    return jnp.dot(a, b, preferred_element_type=f32)


def dot_nt(a, b):
    return lax.dot_general(a, b, (((1,), (1,)), ((), ())), preferred_element_type=f32)


def dot3(a, b, d=dot):
    return d(a[0], b[0]) + d(a[0], b[1]) + d(a[1], b[0])


def advect_chunk(groups, modes, tile, planes, scales, x, spec, small, tabs, scratch):
    ghi, glo, wk, w2 = small
    ch, cl, sh, sl = tabs
    xr, xi, rh, rl, ih, il, col0, acc_re, acc_im, press = scratch
    half = planes // 2
    for g in range(groups):
        lanes = slice(g * modes, (g + 1) * modes)
        cw = wk[0:1, lanes]
        ck = wk[1:2, lanes]
        for i in range(3):
            re = x[g, 0, N2 * i : N2 * i + N2, :]
            im = x[g, 1, N2 * i : N2 * i + N2, :]
            at = slice(PAD * i, PAD * i + N2)
            zt = slice(3 * PAD + PAD * i, 3 * PAD + PAD * i + N2)
            xr[at, lanes] = cw * re
            xi[at, lanes] = cw * im
            xr[zt, lanes] = -ck * im
            xi[zt, lanes] = ck * re
    full = xr[...]
    rh[...], rl[...] = split(full)
    ih[...], il[...] = split(xi[...])
    col0[...] = jnp.broadcast_to(jnp.sum(full * wk[2:3, :], axis=1, keepdims=True), col0.shape)
    acc_re[...] = jnp.zeros_like(acc_re)
    acc_im[...] = jnp.zeros_like(acc_im)
    press[...] = jnp.zeros_like(press)

    def step(q, carry):
        ctab = (ch[q], cl[q])
        stab = (sh[q], sl[q])
        cpart = dot3((rh[...], rl[...]), ctab)
        spart = dot3((ih[...], il[...]), stab)
        lane = lax.broadcasted_iota(jnp.int32, (1, tile), 1) + q * tile
        first = lane == 0
        side_a = cpart - spart
        side_b = jnp.where(first, col0[:, 0:1], cpart + spart)
        plane_b = jnp.where(first, half, planes - lane)
        grad = (ghi[...], glo[...])
        tend = []
        total = jnp.zeros((PAD, tile), f32)
        for side, plane in ((side_a, lane), (side_b, plane_b)):
            inside = ((plane >= 3 * planes // 8) & (plane < 5 * planes // 8)).astype(f32)
            u = [side[PAD * i : PAD * i + PAD] for i in range(3)]
            z = [side[3 * PAD + PAD * i : 4 * PAD + PAD * i] for i in range(3)]
            ux = u[0] * scales[0]
            uy = u[1] * scales[1]
            total = total + u[0] * u[0] * inside
            parts = []
            for i in range(3):
                g = dot3(grad, split(u[i]))
                parts.append(-(ux * g[:PAD] + uy * g[PAD:] + u[2] * z[i]))
            tend.append(jnp.concatenate(parts, axis=0))
        press[...] += total * w2[...]
        plus = split(tend[0] + tend[1])
        minus = split(tend[0] - tend[1])
        acc_re[...] += dot3(plus, ctab, dot_nt)
        acc_im[...] -= dot3(minus, stab, dot_nt)

        @pl.when(q == 0)
        def _():
            acc_re[...] += tend[1][:, 0:1] * (wk[2:3, :] - 1.0)

        return carry

    lax.fori_loop(0, half // tile, step, 0)
    coef = math.sqrt(groups * modes) / planes
    whole = jnp.sum(jnp.sum(press[...], axis=1, keepdims=True), axis=0, keepdims=True)
    tail = jnp.broadcast_to(whole, (ROWS - 3 * N2, modes))
    for g in range(groups):
        lanes = slice(g * modes, (g + 1) * modes)
        for part, acc in ((0, acc_re), (1, acc_im)):
            for i in range(3):
                spec[g, part, N2 * i : N2 * i + N2, :] = (
                    coef * acc[PAD * i : PAD * i + N2, lanes]
                )
            spec[g, part, 3 * N2 : ROWS, :] = tail


def partners(me, groups):
    if groups == 4:
        return [lax.rem(me + 2, 4), 3 - me, me + 1 - 2 * lax.rem(me, 2)]
    return [lax.rem(me + k, groups) for k in range(1, groups)]


def stiffness_line():
    d = derivative_matrix()
    w = np.array(gll_weights)
    k = d.T @ (w[:, None] * d)
    even = np.zeros((5, 5))
    odd = np.zeros((4, 4))
    for i in range(5):
        for j in range(5):
            even[i, j] = k[i, j] if j == 4 else 0.5 * (k[i, j] + k[i, 8 - j])
    for i in range(4):
        for j in range(4):
            odd[i, j] = 0.5 * (k[i, j] - k[i, 8 - j])
    return even, odd


def line_product(v, even, odd):
    s = [v[j] + v[8 - j] for j in range(4)] + [v[4]]
    t = [v[j] - v[8 - j] for j in range(4)]
    ev = [sum(float(even[i, j]) * s[j] for j in range(5)) for i in range(5)]
    od = [sum(float(odd[i, j]) * t[j] for j in range(4)) for i in range(4)]
    return [ev[i] + od[i] for i in range(4)] + [ev[4]] + [ev[i] - od[i] for i in range(3, -1, -1)]


def window_kernel(
    chunks, groups, elems, modes, peers, tile,
    hx_ref, hy_ref, disc_ref, tk_ref, cbase, sbase, rot, ghi, glo, wk, w2, *refs,
):
    vel = refs[:chunks]
    out_ref = refs[chunks]
    (
        r, qb, from_left, from_right, dots, gathered, coef, fs, fr, ds, dr,
        recv, spec, ret, ch, cl, sh, sl, ms, mr, mf_ref, rx_ref, ry_ref, jw_ref, cw_ref, th_ref, *scratch,
    ) = refs[chunks + 1 :]
    me = lax.axis_index("elem")
    slot = lax.axis_index("mode")
    planes = 3 * groups * modes
    face = NPT * elems
    w = gll_weights
    even, odd = stiffness_line()
    mult = [0.5] + [1.0] * 7 + [0.5]
    others = partners(slot, groups)

    barrier = pltpu.get_barrier_semaphore()
    for k in range(1, peers):
        pl.semaphore_signal(
            barrier, inc=1, device_id={"elem": lax.rem(me + k, peers)},
            device_id_type=pl.DeviceIdType.MESH,
        )
    for other in others:
        pl.semaphore_signal(
            barrier, inc=1, device_id={"mode": other}, device_id_type=pl.DeviceIdType.MESH
        )
    pl.semaphore_wait(barrier, peers - 1 + groups - 1)

    def exchange(source, target, n):
        return [
            pltpu.make_async_remote_copy(
                src_ref=source.at[other],
                dst_ref=target.at[slot],
                send_sem=ms.at[n, k],
                recv_sem=mr.at[n, k],
                device_id={"mode": other},
                device_id_type=pl.DeviceIdType.MESH,
            )
            for k, other in enumerate(others)
        ]

    outward = [exchange(vel[c], recv.at[c], c) for c in range(chunks)]
    for copies in outward:
        for copy in copies:
            copy.start()
    for c in range(chunks):
        recv[c, slot] = vel[c][slot]
    xr, xi = scratch[0], scratch[1]
    xr[...] = jnp.zeros_like(xr)
    xi[...] = jnp.zeros_like(xi)
    cos0, sin0 = cbase[...], sbase[...]
    for q in range(planes // 2 // tile):
        cq, sq = rot[:, 2 * q : 2 * q + 1], rot[:, 2 * q + 1 : 2 * q + 2]
        ch[q], cl[q] = split(cos0 * cq - sin0 * sq)
        sh[q], sl[q] = split(sin0 * cq + cos0 * sq)

    shape = (elems, modes)
    for e in range(elems):
        mf_ref[e : e + 1, :] = jnp.full((1, modes), hy_ref[e], f32)
        cw_ref[e : e + 1, :] = jnp.full((1, modes), disc_ref[e], jnp.int32).astype(f32)
    hx, hy, disc = jnp.full(shape, hx_ref[0], f32), mf_ref[...], cw_ref[...]
    index = slot * modes + lax.broadcasted_iota(jnp.int32, shape, 1)
    kz = 8.0 / (groups * modes) * index.astype(f32)
    jacobian = hx * hy / 4.0
    disc_planes = 5 * planes // 8 - 3 * planes // 8
    area = disc_planes * hx * jnp.sum(disc * hy, axis=0, keepdims=True)
    mf_ref[...] = jacobian * (1.0 / time_step + viscosity * kz * kz)
    rx_ref[...] = viscosity * hy / hx
    ry_ref[...] = viscosity * hx / hy
    jw_ref[...] = jacobian / time_step
    cw_ref[...] = disc * jacobian
    th_ref[...] = -(0.5 * thrust_coef * ORDER * time_step) / hx * disc / area

    inward = []
    for c in range(chunks):
        for copy in outward[c]:
            copy.wait()
        scales = (
            2.0 / jnp.full((1, tile), hx_ref[0], f32),
            2.0 / jnp.full((1, tile), hy_ref[slot * chunks + c], f32),
        )
        advect_chunk(
            groups, modes, tile, planes, scales, recv.at[c], spec.at[c],
            (ghi, glo, wk, w2), (ch, cl, sh, sl), scratch,
        )
        copies = exchange(spec.at[c], ret.at[c], chunks + c)
        for copy in copies:
            copy.start()
        ret[c, slot] = spec[c, slot]
        inward.append(copies)

    for c in range(chunks):
        for copy in inward[c]:
            copy.wait()
        for g in range(groups):
            for part in range(2):
                for i in range(3):
                    rows = slice(N2 * i, N2 * i + N2)
                    value = vel[c][g, part, rows, :] + time_step * ret[c, g, part, rows, :]
                    r[2 * i + part, pl.ds(g * chunks + c, N2, stride=elems), :] = value
    pressure = jnp.zeros((1, modes), f32)
    for e in range(elems):
        pressure = pressure + cw_ref[e : e + 1, :] * ret[
            e % chunks, e // chunks, 0, 3 * N2 : 3 * N2 + 1, :
        ]
    push_all = th_ref[...] * pressure

    def row(a, b):
        return pl.ds((a * NPT + b) * elems, elems)

    def joined(line):
        top = line[8] + pltpu.roll(line[0], elems - 1, 0)
        return [pltpu.roll(top, 1, 0)] + line[1:8] + [top]

    def masses(p, carry):
        jw = jw_ref[...]
        push = push_all * tk_ref[slot, pl.ds(p, 1), :]
        for a in range(NPT):
            line = [(r[p, row(a, b), :] + push) * (jw * (w[a] * w[b])) for b in range(NPT)]
            line = joined(line)
            for b in range(NPT):
                r[p, row(a, b), :] = line[b]
        return carry

    lax.fori_loop(0, 6, masses, 0)

    right, left = lax.rem(me + 1, peers), lax.rem(me + peers - 1, peers)

    def face_copies(buffer, n):
        one = pltpu.make_async_remote_copy(
            src_ref=buffer.at[:, pl.ds(8 * face, face), :],
            dst_ref=from_left.at[n],
            send_sem=fs.at[2 * n],
            recv_sem=fr.at[2 * n],
            device_id={"elem": right},
            device_id_type=pl.DeviceIdType.MESH,
        )
        two = pltpu.make_async_remote_copy(
            src_ref=buffer.at[:, pl.ds(0, face), :],
            dst_ref=from_right.at[n],
            send_sem=fs.at[2 * n + 1],
            recv_sem=fr.at[2 * n + 1],
            device_id={"elem": left},
            device_id_type=pl.DeviceIdType.MESH,
        )
        return one, two

    def dot_copies(n):
        copies = []
        for k in range(1, peers):
            copies.append(
                pltpu.make_async_remote_copy(
                    src_ref=dots.at[n],
                    dst_ref=gathered.at[n, k - 1],
                    send_sem=ds.at[n, k - 1],
                    recv_sem=dr.at[n, k - 1],
                    device_id={"elem": lax.rem(me + k, peers)},
                    device_id_type=pl.DeviceIdType.MESH,
                )
            )
        return copies

    def add_faces(buffer, n):
        buffer[:, pl.ds(0, face), :] = buffer[:, pl.ds(0, face), :] + from_left[n]
        buffer[:, pl.ds(8 * face, face), :] = buffer[:, pl.ds(8 * face, face), :] + from_right[n]

    copies = face_copies(r, 0)
    for c in copies:
        c.start()
    for c in copies:
        c.wait()
    add_faces(r, 0)

    def squash(x):
        return jnp.sum(x, axis=0, keepdims=True)

    def apply_first(p, carry):
        mf, rx, ry = mf_ref[...], rx_ref[...], ry_ref[...]
        for b in range(NPT):
            v = [r[p, row(a, b), :] for a in range(NPT)]
            kx = line_product(v, even, odd)
            rxb = rx * w[b]
            mfb = mf * w[b]
            for a in range(NPT):
                qb[p, row(a, b), :] = (mfb * w[a]) * v[a] + rxb * kx[a]
        rr = jnp.zeros((elems, modes), f32)
        pq = jnp.zeros((elems, modes), f32)
        for a in range(NPT):
            v = [r[p, row(a, b), :] for b in range(NPT)]
            ky = line_product(v, even, odd)
            rya = ry * w[a]
            line = [qb[p, row(a, b), :] + rya * ky[b] for b in range(NPT)]
            for b in range(NPT):
                rr = rr + (mult[a] * mult[b]) * (v[b] * v[b])
                pq = pq + v[b] * line[b]
            line = joined(line)
            for b in range(NPT):
                qb[p, row(a, b), :] = line[b]
        dots[0, pl.ds(p, 1), :] = squash(rr)
        dots[0, pl.ds(8 + p, 1), :] = squash(pq)
        return carry

    dots[...] = jnp.zeros_like(dots)
    lax.fori_loop(0, 6, apply_first, 0)
    faces = face_copies(qb, 1)
    sums = dot_copies(0)
    for c in faces + tuple(sums):
        c.start()
    for c in sums:
        c.wait()
    total = dots[0]
    for k in range(peers - 1):
        total = total + gathered[0, k]
    norm = total[0:8]
    alpha = norm / total[8:16]
    coef[0] = alpha
    for c in faces:
        c.wait()
    add_faces(qb, 1)

    def apply_second(p, carry):
        mf, rx, ry = mf_ref[...], rx_ref[...], ry_ref[...]
        al = coef[0, pl.ds(p, 1), :]
        rz = jnp.zeros((elems, modes), f32)
        rr = jnp.zeros((elems, modes), f32)
        for b in range(NPT):
            v = [r[p, row(a, b), :] - al * qb[p, row(a, b), :] for a in range(NPT)]
            kx = line_product(v, even, odd)
            one = jnp.zeros((elems, modes), f32)
            two = jnp.zeros((elems, modes), f32)
            for a in range(NPT):
                qb[p, row(a, b), :] = v[a]
                square = v[a] * v[a]
                one = one + v[a] * kx[a]
                two = two + w[a] * square
                rr = rr + (mult[a] * mult[b]) * square
            rz = rz + w[b] * (rx * one + mf * two)
        for a in range(NPT):
            v = [qb[p, row(a, b), :] for b in range(NPT)]
            ky = line_product(v, even, odd)
            one = jnp.zeros((elems, modes), f32)
            for b in range(NPT):
                one = one + v[b] * ky[b]
            rz = rz + (w[a] * ry) * one
        dots[1, pl.ds(p, 1), :] = squash(rr)
        dots[1, pl.ds(8 + p, 1), :] = squash(rz)
        return carry

    lax.fori_loop(0, 6, apply_second, 0)
    sums = dot_copies(1)
    for c in sums:
        c.start()
    for c in sums:
        c.wait()
    later = dots[1]
    for k in range(peers - 1):
        later = later + gathered[1, k]
    following = later[0:8]
    beta = following / norm
    second = following / (later[8:16] - beta * following / alpha)
    coef[0] = alpha + second * beta
    coef[1] = second

    def finish(p, carry):
        first = coef[0, pl.ds(p, 1), :]
        last = coef[1, pl.ds(p, 1), :]
        r[p] = first * r[p] + last * qb[p]
        return carry

    lax.fori_loop(0, 6, finish, 0)
    for i in range(3):
        for part in range(2):
            for e in range(elems):
                out_ref[i, part, e * N2 : e * N2 + N2, :] = r[
                    2 * i + part, pl.ds(e, N2, stride=elems), :
                ]


def window(vels, scalars, tables):
    chunks = len(vels)
    groups, _, _, modes = vels[0].shape
    elems = groups * chunks
    count = groups * modes
    half = 3 * count // 2
    tile = tables[1].shape[1]
    peers = lax.axis_size("elem")
    body = lambda *refs: window_kernel(chunks, groups, elems, modes, peers, tile, *refs)
    vm = pl.BlockSpec(memory_space=pltpu.VMEM)
    block = (chunks, groups, 2, ROWS, modes)
    table = pltpu.VMEM((half // tile, count, tile), bf16)
    return pl.pallas_call(
        body,
        out_shape=jax.ShapeDtypeStruct((3, 2, elems * N2, modes), f32),
        in_specs=[pl.BlockSpec(memory_space=pltpu.SMEM)] * len(scalars)
        + [vm] * (len(tables) + chunks),
        out_specs=vm,
        scratch_shapes=[
            pltpu.VMEM((6, N2 * elems, modes), f32),
            pltpu.VMEM((6, N2 * elems, modes), f32),
            pltpu.VMEM((2, 6, NPT * elems, modes), f32),
            pltpu.VMEM((2, 6, NPT * elems, modes), f32),
            pltpu.VMEM((2, 16, modes), f32),
            pltpu.VMEM((2, peers - 1, 16, modes), f32),
            pltpu.VMEM((2, 8, modes), f32),
            pltpu.SemaphoreType.DMA((4,)),
            pltpu.SemaphoreType.DMA((4,)),
            pltpu.SemaphoreType.DMA((2, peers - 1)),
            pltpu.SemaphoreType.DMA((2, peers - 1)),
            pltpu.VMEM((chunks, groups, 2, 3 * N2, modes), f32),
            pltpu.VMEM(block, f32),
            pltpu.VMEM(block, f32),
            table,
            table,
            table,
            table,
            pltpu.SemaphoreType.DMA((2 * chunks, groups - 1)),
            pltpu.SemaphoreType.DMA((2 * chunks, groups - 1)),
        ]
        + [pltpu.VMEM((elems, modes), f32)] * 6
        + [
            pltpu.VMEM((6 * PAD, count), f32),
            pltpu.VMEM((6 * PAD, count), f32),
            pltpu.VMEM((6 * PAD, count), bf16),
            pltpu.VMEM((6 * PAD, count), bf16),
            pltpu.VMEM((6 * PAD, count), bf16),
            pltpu.VMEM((6 * PAD, count), bf16),
            pltpu.VMEM((6 * PAD, 128), f32),
            pltpu.VMEM((3 * PAD, count), f32),
            pltpu.VMEM((3 * PAD, count), f32),
            pltpu.VMEM((PAD, tile), f32),
        ],
        compiler_params=pltpu.CompilerParams(
            collective_id=0, has_side_effects=True, vmem_limit_bytes=56 << 20
        ),
    )(*scalars, *tables, *vels)


def on_device(velocity, column_width, row_height, disc_mask):
    groups = lax.axis_size("mode")
    modes = velocity.shape[3]
    count = groups * modes
    planes = 3 * count
    half = planes // 2
    elems = velocity.shape[1] // N2
    chunks = elems // groups

    shaped = velocity.reshape(3, groups, chunks, N2, 2, modes)
    vels = []
    for c in range(chunks):
        piece = jnp.transpose(shaped[:, :, c], (1, 3, 0, 2, 4)).reshape(groups, 2, 3 * N2, modes)
        vels.append(piece)
    derivative = derivative_matrix()
    stacked = np.zeros((2 * PAD, PAD))
    stacked[:N2, :N2] = np.kron(derivative, np.eye(9))
    stacked[PAD : PAD + N2, :N2] = np.kron(np.eye(9), derivative)
    grads = split_host(stacked)
    host_k = np.arange(count)
    weight = np.where(host_k == 0, 1.0, 2.0) / math.sqrt(count)
    wk = np.zeros((8, count), np.float32)
    wk[0] = weight
    wk[1] = weight * (8.0 / count) * host_k
    wk[2] = 1.0 - 2.0 * (host_k % 2)
    wk = jnp.asarray(wk)
    w = np.array(gll_weights)
    tile = 256 if half % 256 == 0 else half
    w2 = np.zeros((PAD, 1), np.float32)
    w2[:N2, 0] = (w[:, None] * w[None, :]).reshape(-1)
    w2 = jnp.asarray(w2)

    turn = 2.0 * np.pi / planes
    base = turn * (host_k[:, None] * np.arange(tile)[None, :] % planes)
    steps = turn * (host_k[:, None] * tile * np.arange(half // tile)[None, :] % planes)
    rotation = np.stack([np.cos(steps), np.sin(steps)], axis=2).reshape(count, -1)
    tables = tuple(jnp.asarray(t.astype(np.float32)) for t in (np.cos(base), np.sin(base), rotation))
    tables = tables + grads + (wk, w2)
    in_planes = np.arange(3 * planes // 8, 5 * planes // 8)
    arg = 2.0 * np.pi * ((host_k[:, None] * in_planes[None, :]) % planes) / planes
    profile = math.sqrt(count) / planes * np.stack([np.cos(arg).sum(1), -np.sin(arg).sum(1)])
    profile = np.concatenate([profile, np.zeros((6, count))])
    profile = profile.astype(np.float32).reshape(8, groups, modes).transpose(1, 0, 2)
    tables = (jnp.asarray(profile),) + tables
    result = window(vels, (column_width, row_height, disc_mask), tables)
    result = result.reshape(3, 2, elems * N2, modes)
    return jnp.transpose(result, (0, 2, 1, 3))


def solution(mesh):
    return jax.shard_map(
        on_device,
        mesh=mesh,
        in_specs=(P(None, "elem", None, "mode"), P("elem"), P(), P("elem")),
        out_specs=P(None, "elem", None, "mode"),
        check_vma=False,
    )
```
